32 devices in a mesh: row: 4 (over x, core), col: 8 (over z, y).
Axes of the slice: x: 2, y: 2, z: 4, core: 2. Of those that a mesh axis runs over, the one named last changes fastest.
Arguments:
- coords: float32 [4, 4096], P(None, ('row', 'col')), may hold values from 0 to 1, as said below
- values: float32 [512, 4096], P(None, ('row', 'col')), may hold values from -6 to 6
- coarse_coords: float32 [4, 512], P(None, ('row', 'col')), may hold values from 0 to 1, as said below
- coarse_values: float32 [512, 512], P(None, ('row', 'col')), may hold values from -6 to 6
- fine_index: int32 [32, 128], P(('row', 'col')), may hold values from 0 to 127, as said below
- coarse_index: int32 [32, 384], P(('row', 'col')), may hold values from 0 to 511, as said below
- log_params: float32 [6], replicated, may hold values from -0.5 to 0.5
Outputs:
- step: float32 [6], replicated
- whitened: float32 [512, 4096], P(None, ('row', 'col'))
The draws below stay inside these ranges and needn't reach their ends.
Inputs may be any that keep to these rules, and one draw needn't show every extreme that they name: `fine_index`: in each row the first 64 entries are distinct, and so are the last 64. `coarse_index`: the entries of each row are distinct; in each row at most 16 entries lie in one tile (j // 16), and some tile holds exactly 16 of them. `coarse_coords`: coarse point j lies in tile j // 16; for tile (r, c) its longitude lies in [c / 8, (c + 1) / 8) and its latitude in [r / 4, (r + 1) / 4), elevation and time in [0, 1). `coords`: fine point p lies in tile p // 128, placed as for the coarse points.
All inputs are finite; a program needn't handle non-finite values.
Results may differ from the reference program's by a relative error of at most 0.0003.
Values sent between devices are 32-bit elements; how exact they have to be, the bound alone decides.
A program may use at most 192 MiB of HBM per device.

```python
import math
import jax
import jax.numpy as jnp
from jax import lax

R = 512
B = 128
FH = 64
COARSE = 384
CP = 16
TOTAL = 4096
CTOTAL = 512
N_ROW = 4
N_COL = 8
DEVICES = 32


def placed_coords(key, per_tile):
    count = DEVICES * per_tile
    unit = jax.random.uniform(key, (4, count), jnp.float32)
    owner = jnp.arange(count, dtype=jnp.int32) // per_tile
    col_pos = (owner % N_COL).astype(jnp.float32)
    row_pos = (owner // N_COL).astype(jnp.float32)
    longitude = (col_pos + unit[0]) / float(N_COL)
    latitude = (row_pos + unit[1]) / float(N_ROW)
    return jnp.stack([longitude, latitude, unit[2], unit[3]])


def draw_coords(key, part):
    return placed_coords(jax.random.fold_in(key, 11), B)


def draw_coarse_coords(key, part):
    return placed_coords(jax.random.fold_in(key, 13), CP)


def draw_fine_index(key, part):
    keys = jax.random.split(jax.random.fold_in(key, 17), 2 * DEVICES)
    picks = jax.vmap(lambda each: jax.random.permutation(each, B)[:FH])(keys)
    return picks.reshape(DEVICES, 2 * FH).astype(jnp.int32)


def one_coarse_row(each):
    limit = min(CP, 2 * ((COARSE + DEVICES - 1) // DEVICES))
    first_key, second_key, third_key = jax.random.split(each, 3)
    forced = jax.random.randint(first_key, (), 0, DEVICES, dtype=jnp.int32)
    pairs = DEVICES * limit
    ranks = jax.random.permutation(second_key, pairs).astype(jnp.int32)
    tile_of = jnp.arange(pairs, dtype=jnp.int32) // limit
    scores = jnp.where(tile_of == forced, ranks - pairs, ranks)
    chosen = jnp.argsort(scores, stable=True)[:COARSE].astype(jnp.int32)
    chosen_tile = chosen // limit
    chosen_slot = chosen % limit
    sub_keys = jax.random.split(third_key, DEVICES)
    inner = jax.vmap(lambda sub: jax.random.permutation(sub, CP))(sub_keys).astype(jnp.int32)
    return chosen_tile * CP + inner[chosen_tile, chosen_slot]


def draw_coarse_index(key, part):
    keys = jax.random.split(jax.random.fold_in(key, 19), DEVICES)
    return jax.vmap(one_coarse_row)(keys).astype(jnp.int32)


def block_scale(rng, dims, pieces, low, top_value):
    def one(dim, blocks):
        steps = jax.random.uniform(jax.random.fold_in(jax.random.fold_in(rng, 6), dim), (blocks,), jnp.float32, low / len(pieces), top_value / len(pieces))
        return jnp.repeat(jnp.exp(steps), dims[dim] // blocks).reshape((-1,) + (1,) * (len(dims) - dim - 1))

    level = one(*pieces[0])
    for cut in pieces[1:]:
        level = level * one(*cut)
    return level


def normal_values(key, shape, deviation, bound, pieces=(), kind=jnp.bfloat16):
    values = deviation * jax.random.normal(key, shape, jnp.float32)
    if pieces:
        values = values * block_scale(key, shape, pieces, -0.22, 0.18)
    return jnp.clip(values, -bound, bound).astype(kind)


def setup_inputs(seed: int = 0) -> dict:
    key_of = jax.random.split(jax.random.key(seed), 8)
    coords = draw_coords(jax.random.fold_in(key_of[7], 71), 0)
    values = normal_values(key_of[1], (R, TOTAL), 1.0, 6.0, ((1, 32),), jnp.float32)
    coarse_coords = draw_coarse_coords(jax.random.fold_in(key_of[7], 71), 0)
    coarse_values = normal_values(key_of[3], (R, CTOTAL), 1.0, 6.0, ((1, 32),), jnp.float32)
    fine_index = draw_fine_index(jax.random.fold_in(key_of[7], 71), 0)
    coarse_index = draw_coarse_index(jax.random.fold_in(key_of[7], 71), 0)
    log_params = jnp.clip(jax.random.uniform(key_of[6], (6,), jnp.float32, -0.5, 0.5), -0.5, 0.5)
    return dict(coords=coords, values=values, coarse_coords=coarse_coords, coarse_values=coarse_values, fine_index=fine_index, coarse_index=coarse_index, log_params=log_params)


HIGH = lax.Precision.HIGHEST
ROOT_FIVE = math.sqrt(5.0)
NUGGET = 0.2
RANGE_BASE = (0.5, 0.5, 0.5, 0.5)

def local_covariance(joint_coords, live, theta):
    count = joint_coords.shape[1]
    scale = jnp.exp(theta[1:5]) * jnp.array(RANGE_BASE)
    scaled = joint_coords / scale[:, None]
    diff = scaled[:, :, None] - scaled[:, None, :]
    squares = diff * diff
    dist = jnp.sqrt(lax.optimization_barrier(jnp.sum(squares, axis=0)))
    root = ROOT_FIVE * dist
    decay = jnp.exp(-root)
    variance = jnp.exp(theta[0])
    kernel = variance * (1.0 + root + root * root / 3.0) * decay
    common = variance * (5.0 / 3.0) * (1.0 + root) * decay
    paired = live[:, None] * live[None, :]
    ident = jnp.eye(count, dtype=jnp.float32)
    nugget = NUGGET * jnp.exp(theta[5])
    cov = paired * kernel + (live * nugget + 1.0 - live)[:, None] * ident
    derivs = jnp.concatenate([(paired * kernel)[None], (paired * common)[None] * squares, ((live * nugget)[:, None] * ident)[None]], axis=0)
    return (cov, derivs)

def fisher_terms(cov, derivs, lead, reps):
    count = cov.shape[0]
    ident = jnp.eye(count, dtype=jnp.float32)
    factor = jnp.linalg.cholesky(cov)
    inverse = jax.scipy.linalg.solve_triangular(factor, ident, lower=True)
    joint_prec = jnp.dot(inverse.T, inverse, precision=HIGH)
    lead_inv = inverse[:lead, :lead]
    lead_prec = jnp.dot(lead_inv.T, lead_inv, precision=HIGH)
    joint_prod = jnp.einsum('ab,ibc->iac', joint_prec, derivs, precision=HIGH)
    lead_prod = jnp.einsum('ab,ibc->iac', lead_prec, derivs[:, :lead, :lead], precision=HIGH)
    joint_fish = jnp.einsum('iab,jba->ij', joint_prod, joint_prod, precision=HIGH)
    lead_fish = jnp.einsum('iab,jba->ij', lead_prod, lead_prod, precision=HIGH)
    fisher = reps * 0.5 * (joint_fish - lead_fish)
    traces = jnp.trace(joint_prod, axis1=1, axis2=2) - jnp.trace(lead_prod, axis1=1, axis2=2)
    return (inverse, fisher, traces)

def score_terms(inverse, derivs, joint_values, traces, lead, reps):
    white = jnp.dot(joint_values, inverse.T, precision=HIGH)
    alpha = jnp.dot(white, inverse, precision=HIGH)
    lead_alpha = jnp.dot(white[:, :lead], inverse[:lead, :lead], precision=HIGH)
    joint_quad = lax.optimization_barrier(jnp.sum(jnp.einsum('rn,inm->irm', alpha, derivs, precision=HIGH) * alpha[None], axis=(1, 2)))
    lead_quad = lax.optimization_barrier(jnp.sum(jnp.einsum('rn,inm->irm', lead_alpha, derivs[:, :lead, :lead], precision=HIGH) * lead_alpha[None], axis=(1, 2)))
    grad = 0.5 * (joint_quad - lead_quad) - 0.5 * reps * traces
    return (grad, white[:, lead:])

def reference(coords, values, coarse_coords, coarse_values, fine_index, coarse_index, log_params):
    lead = COARSE + 2 * FH
    tile_coords = coords.reshape(4, DEVICES, B)
    tile_values = values.reshape(R, DEVICES, B)

    def one_block(device):
        row_pos = device // N_COL
        col_pos = device % N_COL
        upper = jnp.maximum(device - N_COL, 0).astype(jnp.int32)
        left = (row_pos * N_COL + (col_pos + N_COL - 1) % N_COL).astype(jnp.int32)
        upper_live = (row_pos > 0).astype(jnp.float32)
        picks = fine_index[device]
        wanted = coarse_index[device]
        upper_coords = jnp.take(jnp.take(tile_coords, upper, axis=1), picks[:FH], axis=1) * upper_live
        upper_values = jnp.take(jnp.take(tile_values, upper, axis=1), picks[:FH], axis=1) * upper_live
        left_coords = jnp.take(jnp.take(tile_coords, left, axis=1), picks[FH:], axis=1)
        left_values = jnp.take(jnp.take(tile_values, left, axis=1), picks[FH:], axis=1)
        joint_coords = jnp.concatenate([jnp.take(coarse_coords, wanted, axis=1), upper_coords, left_coords, jnp.take(tile_coords, device, axis=1)], axis=1)
        joint_values = jnp.concatenate([jnp.take(coarse_values, wanted, axis=1), upper_values, left_values, jnp.take(tile_values, device, axis=1)], axis=1)
        live = jnp.concatenate([jnp.ones((COARSE,), jnp.float32), upper_live * jnp.ones((FH,), jnp.float32), jnp.ones((FH + B,), jnp.float32)])
        cov, derivs = local_covariance(joint_coords, live, log_params)
        inverse, fisher, traces = fisher_terms(cov, derivs, lead, R)
        grad, white = score_terms(inverse, derivs, joint_values, traces, lead, R)
        return (grad, fisher, white)
    grads, fishers, whites = lax.map(one_block, jnp.arange(DEVICES, dtype=jnp.int32))
    grad = lax.optimization_barrier(jnp.sum(grads, axis=0))
    fisher = lax.optimization_barrier(jnp.sum(fishers, axis=0))
    step = jax.scipy.linalg.cho_solve((jnp.linalg.cholesky(fisher), True), grad)
    whitened = jnp.transpose(whites, (1, 0, 2)).reshape(R, DEVICES * B)
    return (step, whitened)
```

```python
import functools
import math

import jax
import jax.numpy as jnp
from jax import lax
from jax.experimental import pallas as pl
from jax.experimental.pallas import tpu as pltpu
from jax.sharding import PartitionSpec as P

HIGH = lax.Precision.HIGHEST
ROOT_FIVE = math.sqrt(5.0)
NUGGET = 0.2
RANGE_BASE = (0.5, 0.5, 0.5, 0.5)
BLK = 128
PAN = 16
F32 = jnp.float32


def mm(a, b):
    return jnp.dot(a, b, precision=HIGH, preferred_element_type=F32)


def mm_tn(a, b):
    return lax.dot_general(
        a, b, (((0,), (0,)), ((), ())), precision=HIGH, preferred_element_type=F32
    )


def rows(b):
    return pl.ds(b * BLK, BLK)


def inverse_factor(s_ref):
    row = lax.broadcasted_iota(jnp.int32, (PAN, BLK), 0)
    lane = lax.broadcasted_iota(jnp.int32, (PAN, BLK), 1)

    def panel(p, carry):
        start = pl.multiple_of(p * PAN, PAN)
        xa = s_ref[pl.ds(start, PAN), :BLK]
        xb = s_ref[pl.ds(start, PAN), BLK:]
        turned = pltpu.roll(xa, lax.rem(BLK - start, BLK), 1)
        cols = [jnp.broadcast_to(turned[:, j : j + 1], (PAN, BLK)) for j in range(PAN)]
        for k in range(PAN):
            inv = lax.rsqrt(cols[k][k : k + 1, :])
            low = cols[k] * inv
            for j in range(k + 1, PAN):
                cols[j] = cols[j] - low * low[j : j + 1, :]
            below = jnp.where(row > k, low, 0.0)
            ua = xa[k : k + 1, :] * inv
            ub = xb[k : k + 1, :] * inv
            xa = jnp.where(row == k, ua, xa - below * ua)
            xb = jnp.where(row == k, ub, xb - below * ub)
        s_ref[pl.ds(start, PAN), :BLK] = xa
        s_ref[pl.ds(start, PAN), BLK:] = xb
        tail = jnp.where(lane >= start + PAN, xa, 0.0)
        s_ref[...] -= mm_tn(tail, jnp.concatenate([xa, xb], axis=1))
        return carry

    lax.fori_loop(0, BLK // PAN, panel, 0)


def forward(u_ref, inv_ref, x_ref, count):
    for b in range(count):
        part = x_ref[rows(b), :]
        if b:
            part = part - mm_tn(u_ref[: b * BLK, b * BLK : (b + 1) * BLK], x_ref[: b * BLK, :])
        x_ref[rows(b), :] = mm(inv_ref[rows(b), :], part)


def model_kernel(reps, scal, xr, xc, u_ref, inv_ref, wt_ref, h_ref, z_ref, f_ref, c_ref, s_ref):
    n = xr.shape[1]
    nb = n // BLK
    lead = n - BLK
    lb = nb - 1
    variance, nugget = scal[0], scal[1]

    def cover(r, carry):
        start = pl.multiple_of(r * 64, 64)
        here = pl.ds(start, 64)
        total = None
        for k in range(4):
            diff = xc[here, k : k + 1] - xr[k : k + 1, :]
            total = diff * diff if total is None else total + diff * diff
        live_c = xc[here, 4:5]
        paired = live_c * xr[4:5, :]
        root = ROOT_FIVE * jnp.sqrt(total)
        decay = jnp.exp(-root) * (variance * paired)
        ident = (
            lax.broadcasted_iota(jnp.int32, (64, n), 0) + start
            == lax.broadcasted_iota(jnp.int32, (64, n), 1)
        )
        u_ref[here, :] = (1.0 + root + root * root / 3.0) * decay + jnp.where(
            ident, live_c * nugget + 1.0 - live_c, 0.0
        )
        c_ref[here, :] = (5.0 / 3.0) * (1.0 + root) * decay
        return carry

    lax.fori_loop(0, n // 64, cover, 0)

    eye = (
        lax.broadcasted_iota(jnp.int32, (BLK, BLK), 0)
        == lax.broadcasted_iota(jnp.int32, (BLK, BLK), 1)
    ).astype(F32)
    for b in range(nb):
        s_ref[:, :BLK] = u_ref[rows(b), b * BLK : (b + 1) * BLK]
        s_ref[:, BLK:] = eye
        inverse_factor(s_ref)
        inv = s_ref[:, BLK:]
        inv_ref[rows(b), :] = inv
        if b + 1 < nb:
            rest = (b + 1) * BLK
            u_ref[rows(b), rest:] = mm(inv, u_ref[rows(b), rest:])
            for i in range(b + 1, nb):
                u_ref[rows(i), i * BLK :] -= mm_tn(
                    u_ref[rows(b), i * BLK : (i + 1) * BLK], u_ref[rows(b), i * BLK :]
                )

    last = inv_ref[rows(lb), :]
    wt_ref[rows(lb), :] = last.T
    right = -mm(u_ref[:lead, lead:], last.T)
    for b in range(lb - 1, -1, -1):
        part = right[b * BLK : (b + 1) * BLK, :]
        if b + 1 < lb:
            part = part - mm(u_ref[rows(b), (b + 1) * BLK : lead], wt_ref[(b + 1) * BLK : lead, :])
        wt_ref[rows(b), :] = mm_tn(inv_ref[rows(b), :], part)

    wt = wt_ref[...]

    def slopes(r, carry):
        here = pl.ds(pl.multiple_of(r * BLK, BLK), BLK)
        for k in range(4):
            diff = xc[here, k : k + 1] - xr[k : k + 1, :]
            h_ref[here, k * BLK : (k + 1) * BLK] = mm(c_ref[here, :] * (diff * diff), wt)
        h_ref[here, 4 * BLK :] = nugget * wt_ref[here, :]
        return carry

    lax.fori_loop(0, nb, slopes, 0)
    z_ref[...] = mm_tn(wt, h_ref[...])
    forward(u_ref, inv_ref, h_ref, lb)

    def h_of(i):
        i = 4 if i in (0, 5) else i - 1
        return h_ref[:lead, i * BLK : (i + 1) * BLK]

    def z_of(i):
        if i == 0:
            return eye - z_ref[:, 4 * BLK :]
        return z_ref[:, (i - 1) * BLK : i * BLK]

    row8 = lax.broadcasted_iota(jnp.int32, (8, BLK), 0)
    lane8 = lax.broadcasted_iota(jnp.int32, (8, BLK), 1)
    out = jnp.zeros((8, BLK), F32)
    for i in range(6):
        for j in range(i, 6):
            sign = -2.0 if (i == 0) != (j == 0) else 2.0
            both = sign * jnp.sum(h_of(i) * h_of(j), axis=0, keepdims=True)
            both = both + jnp.sum(z_of(i) * z_of(j), axis=0, keepdims=True)
            value = (0.5 * reps) * jnp.sum(both, axis=1, keepdims=True)
            spot = (row8 == i) & (lane8 == j) | (row8 == j) & (lane8 == i)
            out = out + jnp.where(spot, value, 0.0)
    f_ref[...] = out


def data_kernel(
    coarse, upper, left, own, cidx, fidx, u_ref, inv_ref, wt_ref, h_ref, z_ref, f_ref,
    white_ref, out_ref, m_ref,
):
    reps = own.shape[0]
    n = wt_ref.shape[0]
    lead = n - BLK
    nc = cidx.shape[1]
    half = fidx.shape[1] // 2

    def onehot(index, count):
        return (
            lax.broadcasted_iota(jnp.int32, (count, index.shape[1]), 0) == index
        ).astype(F32)

    hot_c = onehot(cidx[...], coarse.shape[1])
    hot_u = onehot(fidx[:, :half], upper.shape[1])
    hot_l = onehot(fidx[:, half:], left.shape[1])
    white = mm(coarse[...], mm(hot_c, wt_ref[:nc, :]))
    white = white + mm(upper[...], mm(hot_u, wt_ref[nc : nc + half, :]))
    white = white + mm(left[...], mm(hot_l, wt_ref[nc + half : lead, :]))
    white = white + mm(own[...], wt_ref[lead:, :])
    white_ref[...] = white
    m_ref[:nc, :] = mm_tn(hot_c, mm_tn(coarse[...], white))
    m_ref[nc : nc + half, :] = mm_tn(hot_u, mm_tn(upper[...], white))
    m_ref[nc + half :, :] = mm_tn(hot_l, mm_tn(left[...], white))
    forward(u_ref, inv_ref, m_ref, lead // BLK)
    gram = mm_tn(white, white)
    eye = (
        lax.broadcasted_iota(jnp.int32, (BLK, BLK), 0)
        == lax.broadcasted_iota(jnp.int32, (BLK, BLK), 1)
    ).astype(F32)
    weight = 0.5 * gram - (0.5 * reps) * eye
    row8 = lax.broadcasted_iota(jnp.int32, (8, BLK), 0)
    lane8 = lax.broadcasted_iota(jnp.int32, (8, BLK), 1)
    out = f_ref[...]
    for i in range(6):
        at = 4 if i in (0, 5) else i - 1
        lead_part = jnp.sum(m_ref[...] * h_ref[:lead, at * BLK : (at + 1) * BLK], axis=0, keepdims=True)
        z = z_ref[:, at * BLK : (at + 1) * BLK]
        if i == 0:
            z = eye - z
            lead_part = -lead_part
        both = lead_part + jnp.sum(weight * z, axis=0, keepdims=True)
        value = jnp.sum(both, axis=1, keepdims=True)
        out = out + jnp.where((row8 == i) & (lane8 == 6), value, 0.0)
    out_ref[...] = out


def solve_kernel(x_ref, out_ref):
    out_ref[...] = eliminated(x_ref[...])


def eliminated(x):
    row8 = lax.broadcasted_iota(jnp.int32, (8, BLK), 0)
    for k in range(6):
        top = x[k : k + 1, :] / x[k : k + 1, k : k + 1]
        x = jnp.where(row8 == k, top, x - x[:, k : k + 1] * top)
    return x


def vmem(count):
    return [pl.BlockSpec(memory_space=pltpu.VMEM)] * count


def shape(*dims):
    return jax.ShapeDtypeStruct(dims, F32)


def body(coords, values, coarse_coords, coarse_values, fine_index, coarse_index, log_params):
    half = fine_index.shape[1] // 2
    reps = values.shape[0]
    block = coords.shape[1]
    nc = coarse_index.shape[1]
    n = nc + 2 * half + block
    n_row, n_col = lax.axis_size("row"), lax.axis_size("col")
    down = [(i, i + 1) for i in range(n_row - 1)]
    across = [((i - 1) % n_col, i) for i in range(n_col)]
    all_coords = lax.all_gather(coarse_coords, ("row", "col"), axis=1, tiled=True)
    upper_coords = lax.ppermute(coords, "row", down)
    left_coords = lax.ppermute(coords, "col", across)
    upper_values = lax.ppermute(values, "row", down)
    left_values = lax.ppermute(values, "col", across)
    all_values = lax.all_gather(coarse_values, ("row", "col"), axis=1, tiled=True)

    def pick(array, index):
        hot = (index[None, :] == jnp.arange(array.shape[1], dtype=jnp.int32)[:, None]).astype(F32)
        return jnp.dot(array, hot, precision=HIGH)

    upper_live = (lax.axis_index("row") > 0).astype(F32)
    joint = jnp.concatenate(
        [
            pick(all_coords, coarse_index[0]),
            pick(upper_coords, fine_index[0, :half]),
            pick(left_coords, fine_index[0, half:]),
            coords,
        ],
        axis=1,
    )
    scale = jnp.exp(log_params[1:5]) * jnp.array(RANGE_BASE, F32)
    live = jnp.concatenate(
        [jnp.ones((nc,), F32), upper_live * jnp.ones((half,), F32), jnp.ones((half + block,), F32)]
    )
    xr = jnp.concatenate([joint / scale[:, None], live[None], jnp.zeros((3, n), F32)], axis=0)
    scal = jnp.stack([jnp.exp(log_params[0]), NUGGET * jnp.exp(log_params[5])])
    lead = n - block
    u, inv, wt, h, z, fish = pl.pallas_call(
        functools.partial(model_kernel, float(reps)),
        out_shape=[
            shape(n, n), shape(n, BLK), shape(n, BLK), shape(n, 5 * BLK), shape(BLK, 5 * BLK),
            shape(8, BLK),
        ],
        in_specs=[pl.BlockSpec(memory_space=pltpu.SMEM)] + vmem(2),
        out_specs=vmem(6),
        scratch_shapes=[pltpu.VMEM((n, n), F32), pltpu.VMEM((BLK, 2 * BLK), F32)],
        compiler_params=pltpu.CompilerParams(vmem_limit_bytes=40 * 1024 * 1024),
        cost_estimate=pl.CostEstimate(
            flops=60_000_000_000, bytes_accessed=8_000_000, transcendentals=2 * n * n
        ),
    )(scal, xr, xr.T)
    white, terms = pl.pallas_call(
        data_kernel,
        out_shape=[shape(reps, BLK), shape(8, BLK)],
        in_specs=vmem(12),
        out_specs=vmem(2),
        scratch_shapes=[pltpu.VMEM((lead, BLK), F32)],
        compiler_params=pltpu.CompilerParams(vmem_limit_bytes=40 * 1024 * 1024),
    )(all_values, upper_values, left_values, values, coarse_index, fine_index, u, inv, wt, h, z, fish)
    total = lax.psum(terms, ("row", "col"))
    solved = pl.pallas_call(
        solve_kernel, out_shape=shape(8, BLK), in_specs=vmem(1), out_specs=vmem(1)[0]
    )(total)
    return (solved[:6, 6], white)


def solution(mesh):
    in_specs = (
        P(None, ("row", "col")),
        P(None, ("row", "col")),
        P(None, ("row", "col")),
        P(None, ("row", "col")),
        P(("row", "col"), None),
        P(("row", "col"), None),
        P(),
    )
    out_specs = (P(), P(None, ("row", "col")))
    return jax.shard_map(body, mesh=mesh, in_specs=in_specs, out_specs=out_specs, check_vma=False)
```

```python
import functools
import math

import jax
import jax.numpy as jnp
from jax import lax
from jax.experimental import pallas as pl
from jax.experimental.pallas import tpu as pltpu
from jax.sharding import PartitionSpec as P

HIGH = lax.Precision.HIGHEST
ROOT_FIVE = math.sqrt(5.0)
NUGGET = 0.2
RANGE_BASE = (0.5, 0.5, 0.5, 0.5)
BLK = 128
PAN = 16
F32 = jnp.float32


def mm(a, b):
    return jnp.dot(a, b, precision=HIGH, preferred_element_type=F32)


def mm_tn(a, b):
    return lax.dot_general(
        a, b, (((0,), (0,)), ((), ())), precision=HIGH, preferred_element_type=F32
    )


def rows(b):
    return pl.ds(b * BLK, BLK)


def inverse_factor(s_ref):
    row = lax.broadcasted_iota(jnp.int32, (PAN, BLK), 0)
    lane = lax.broadcasted_iota(jnp.int32, (PAN, BLK), 1)

    def panel(p, carry):
        start = pl.multiple_of(p * PAN, PAN)
        xa = s_ref[pl.ds(start, PAN), :BLK]
        xb = s_ref[pl.ds(start, PAN), BLK:]
        turned = pltpu.roll(xa, lax.rem(BLK - start, BLK), 1)
        cols = [jnp.broadcast_to(turned[:, j : j + 1], (PAN, BLK)) for j in range(PAN)]
        for k in range(PAN):
            inv = lax.rsqrt(cols[k][k : k + 1, :])
            low = cols[k] * inv
            for j in range(k + 1, PAN):
                cols[j] = cols[j] - low * low[j : j + 1, :]
            below = jnp.where(row > k, low, 0.0)
            ua = xa[k : k + 1, :] * inv
            ub = xb[k : k + 1, :] * inv
            xa = jnp.where(row == k, ua, xa - below * ua)
            xb = jnp.where(row == k, ub, xb - below * ub)
        s_ref[pl.ds(start, PAN), :BLK] = xa
        s_ref[pl.ds(start, PAN), BLK:] = xb
        tail = jnp.where(lane >= start + PAN, xa, 0.0)
        s_ref[...] -= mm_tn(tail, jnp.concatenate([xa, xb], axis=1))
        return carry

    lax.fori_loop(0, BLK // PAN, panel, 0)


def forward(u_ref, inv_ref, x_ref, count):
    for b in range(count):
        part = x_ref[rows(b), :]
        if b:
            part = part - mm_tn(u_ref[: b * BLK, b * BLK : (b + 1) * BLK], x_ref[: b * BLK, :])
        x_ref[rows(b), :] = mm(inv_ref[rows(b), :], part)


def model_kernel(
    reps, per_tile, scal, where, held, cidx, fidx, u_ref, inv_ref, wt_ref, h_ref, z_ref, f_ref,
    c_ref, s_ref, xr, xc,
):
    n = xr.shape[1]
    nb = n // BLK
    lead = n - BLK
    lb = nb - 1
    nc = cidx.shape[1]
    half = fidx.shape[1] // 2
    count = held.shape[0]
    variance, nugget = scal[0], scal[1]
    row8 = lax.broadcasted_iota(jnp.int32, (8, BLK), 0)
    scale = sum(jnp.where(row8 == k, scal[2 + k], 0.0) for k in range(4))[:, :1]

    wanted = cidx[...]
    tile = wanted // per_tile
    spot = wanted - tile * per_tile
    hot = (lax.broadcasted_iota(jnp.int32, (BLK, nc), 0) == spot).astype(F32)
    spread = mm(held[...].reshape(count * 8, BLK), hot).reshape(count, 8, nc)
    owner = lax.broadcasted_iota(jnp.int32, (count, 8, nc), 0)
    coarse = jnp.sum(jnp.where(owner == tile[None], spread, 0.0), axis=0)
    xr[:, :nc] = pltpu.roll(coarse, 4, 0) * scale

    def neighbour(device, index):
        pick = (lax.broadcasted_iota(jnp.int32, (BLK, half), 0) == index).astype(F32)
        return mm(held[device], pick) * scale

    alive = jnp.where(where[1] > 0, 1.0, 0.0)
    near = jnp.concatenate(
        [neighbour(where[2], fidx[:, :half]) * alive, neighbour(where[3], fidx[:, half:])], axis=1
    )
    xr[:, nc:lead] = near
    xr[:, lead:] = held[where[0]] * scale
    point = lax.broadcasted_iota(jnp.int32, (1, n), 1)
    xr[4:5, :] = jnp.where((point >= nc) & (point < nc + half), alive, 1.0)
    for b in range(nb):
        xc[rows(b), :] = xr[:, b * BLK : (b + 1) * BLK].T

    def cover(r, carry):
        start = pl.multiple_of(r * 64, 64)
        here = pl.ds(start, 64)
        total = None
        for k in range(4):
            diff = xc[here, k : k + 1] - xr[k : k + 1, :]
            total = diff * diff if total is None else total + diff * diff
        live_c = xc[here, 4:5]
        paired = live_c * xr[4:5, :]
        root = ROOT_FIVE * jnp.sqrt(total)
        decay = jnp.exp(-root) * (variance * paired)
        ident = (
            lax.broadcasted_iota(jnp.int32, (64, n), 0) + start
            == lax.broadcasted_iota(jnp.int32, (64, n), 1)
        )
        u_ref[here, :] = (1.0 + root + root * root / 3.0) * decay + jnp.where(
            ident, live_c * nugget + 1.0 - live_c, 0.0
        )
        c_ref[here, :] = (5.0 / 3.0) * (1.0 + root) * decay
        return carry

    lax.fori_loop(0, n // 64, cover, 0)

    eye = (
        lax.broadcasted_iota(jnp.int32, (BLK, BLK), 0)
        == lax.broadcasted_iota(jnp.int32, (BLK, BLK), 1)
    ).astype(F32)
    for b in range(nb):
        s_ref[:, :BLK] = u_ref[rows(b), b * BLK : (b + 1) * BLK]
        s_ref[:, BLK:] = eye
        inverse_factor(s_ref)
        inv = s_ref[:, BLK:]
        inv_ref[rows(b), :] = inv
        if b + 1 < nb:
            rest = (b + 1) * BLK
            u_ref[rows(b), rest:] = mm(inv, u_ref[rows(b), rest:])
            for i in range(b + 1, nb):
                u_ref[rows(i), i * BLK :] -= mm_tn(
                    u_ref[rows(b), i * BLK : (i + 1) * BLK], u_ref[rows(b), i * BLK :]
                )

    last = inv_ref[rows(lb), :]
    wt_ref[rows(lb), :] = last.T
    right = -mm(u_ref[:lead, lead:], last.T)
    for b in range(lb - 1, -1, -1):
        part = right[b * BLK : (b + 1) * BLK, :]
        if b + 1 < lb:
            part = part - mm(u_ref[rows(b), (b + 1) * BLK : lead], wt_ref[(b + 1) * BLK : lead, :])
        wt_ref[rows(b), :] = mm_tn(inv_ref[rows(b), :], part)

    wt = wt_ref[...]

    def slopes(r, carry):
        here = pl.ds(pl.multiple_of(r * BLK, BLK), BLK)
        for k in range(4):
            diff = xc[here, k : k + 1] - xr[k : k + 1, :]
            h_ref[here, k * BLK : (k + 1) * BLK] = mm(c_ref[here, :] * (diff * diff), wt)
        h_ref[here, 4 * BLK :] = nugget * wt_ref[here, :]
        return carry

    lax.fori_loop(0, nb, slopes, 0)
    z_ref[...] = mm_tn(wt, h_ref[...])
    forward(u_ref, inv_ref, h_ref, lb)

    def h_of(i):
        i = 4 if i in (0, 5) else i - 1
        return h_ref[:lead, i * BLK : (i + 1) * BLK]

    def z_of(i):
        if i == 0:
            return eye - z_ref[:, 4 * BLK :]
        return z_ref[:, (i - 1) * BLK : i * BLK]

    lane8 = lax.broadcasted_iota(jnp.int32, (8, BLK), 1)
    out = jnp.zeros((8, BLK), F32)
    for i in range(6):
        for j in range(i, 6):
            sign = -2.0 if (i == 0) != (j == 0) else 2.0
            both = sign * jnp.sum(h_of(i) * h_of(j), axis=0, keepdims=True)
            both = both + jnp.sum(z_of(i) * z_of(j), axis=0, keepdims=True)
            value = (0.5 * reps) * jnp.sum(both, axis=1, keepdims=True)
            spot = (row8 == i) & (lane8 == j) | (row8 == j) & (lane8 == i)
            out = out + jnp.where(spot, value, 0.0)
    f_ref[...] = out


def data_kernel(
    coarse, upper, left, own, cidx, fidx, u_ref, inv_ref, wt_ref, h_ref, z_ref, f_ref,
    white_ref, out_ref, m_ref,
):
    reps = own.shape[0]
    n = wt_ref.shape[0]
    lead = n - BLK
    nc = cidx.shape[1]
    half = fidx.shape[1] // 2

    def onehot(index, count):
        return (
            lax.broadcasted_iota(jnp.int32, (count, index.shape[1]), 0) == index
        ).astype(F32)

    hot_c = onehot(cidx[...], coarse.shape[1])
    hot_u = onehot(fidx[:, :half], upper.shape[1])
    hot_l = onehot(fidx[:, half:], left.shape[1])
    white = mm(coarse[...], mm(hot_c, wt_ref[:nc, :]))
    white = white + mm(upper[...], mm(hot_u, wt_ref[nc : nc + half, :]))
    white = white + mm(left[...], mm(hot_l, wt_ref[nc + half : lead, :]))
    white = white + mm(own[...], wt_ref[lead:, :])
    white_ref[...] = white
    m_ref[:nc, :] = mm_tn(hot_c, mm_tn(coarse[...], white))
    m_ref[nc : nc + half, :] = mm_tn(hot_u, mm_tn(upper[...], white))
    m_ref[nc + half :, :] = mm_tn(hot_l, mm_tn(left[...], white))
    forward(u_ref, inv_ref, m_ref, lead // BLK)
    gram = mm_tn(white, white)
    eye = (
        lax.broadcasted_iota(jnp.int32, (BLK, BLK), 0)
        == lax.broadcasted_iota(jnp.int32, (BLK, BLK), 1)
    ).astype(F32)
    weight = 0.5 * gram - (0.5 * reps) * eye
    row8 = lax.broadcasted_iota(jnp.int32, (8, BLK), 0)
    lane8 = lax.broadcasted_iota(jnp.int32, (8, BLK), 1)
    out = f_ref[...]
    for i in range(6):
        at = 4 if i in (0, 5) else i - 1
        lead_part = jnp.sum(m_ref[...] * h_ref[:lead, at * BLK : (at + 1) * BLK], axis=0, keepdims=True)
        z = z_ref[:, at * BLK : (at + 1) * BLK]
        if i == 0:
            z = eye - z
            lead_part = -lead_part
        both = lead_part + jnp.sum(weight * z, axis=0, keepdims=True)
        value = jnp.sum(both, axis=1, keepdims=True)
        out = out + jnp.where((row8 == i) & (lane8 == 6), value, 0.0)
    out_ref[...] = out


def exchange(x_ref, held, send_sem, recv_sem):
    n_row, n_col = lax.axis_size("row"), lax.axis_size("col")
    count = n_row * n_col
    me = lax.axis_index("row") * n_col + lax.axis_index("col")

    def place(device):
        return {"row": device // n_col, "col": lax.rem(device, n_col)}

    barrier = pltpu.get_barrier_semaphore()

    def greet(d, carry):
        pl.semaphore_signal(
            barrier, inc=1, device_id=place(lax.rem(me + d, count)),
            device_id_type=pl.DeviceIdType.MESH,
        )
        return carry

    lax.fori_loop(1, count, greet, 0)
    pl.semaphore_wait(barrier, count - 1)

    def copy(d, slot):
        return pltpu.make_async_remote_copy(
            src_ref=x_ref, dst_ref=held.at[slot], send_sem=send_sem.at[d],
            recv_sem=recv_sem.at[d], device_id=place(lax.rem(me + d, count)),
            device_id_type=pl.DeviceIdType.MESH,
        )

    def push(d, carry):
        copy(d, me).start()
        return carry

    def settle(d, carry):
        copy(d, lax.rem(me - d + count, count)).wait()
        return carry

    lax.fori_loop(1, count, push, 0)
    held[me] = x_ref[...]
    lax.fori_loop(1, count, settle, 0)


def share_kernel(x_ref, out_ref, held, send_sem, recv_sem):
    exchange(x_ref, held, send_sem, recv_sem)
    out_ref[...] = held[...]


def solve_kernel(x_ref, out_ref, held, send_sem, recv_sem):
    exchange(x_ref, held, send_sem, recv_sem)
    out_ref[...] = eliminated(jnp.sum(held[...], axis=0))


def exchanged(kernel, out_shape, number, payload):
    count = lax.axis_size("row") * lax.axis_size("col")
    return pl.pallas_call(
        kernel,
        out_shape=out_shape,
        in_specs=vmem(1),
        out_specs=vmem(1)[0],
        scratch_shapes=[
            pltpu.VMEM((count, 8, BLK), F32),
            pltpu.SemaphoreType.DMA((count,)),
            pltpu.SemaphoreType.DMA((count,)),
        ],
        compiler_params=pltpu.CompilerParams(collective_id=number, has_side_effects=True),
    )(payload)


def eliminated(x):
    row8 = lax.broadcasted_iota(jnp.int32, (8, BLK), 0)
    for k in range(6):
        top = x[k : k + 1, :] / x[k : k + 1, k : k + 1]
        x = jnp.where(row8 == k, top, x - x[:, k : k + 1] * top)
    return x


def vmem(count):
    return [pl.BlockSpec(memory_space=pltpu.VMEM)] * count


def shape(*dims):
    return jax.ShapeDtypeStruct(dims, F32)


def body(coords, values, coarse_coords, coarse_values, fine_index, coarse_index, log_params):
    half = fine_index.shape[1] // 2
    reps = values.shape[0]
    block = coords.shape[1]
    nc = coarse_index.shape[1]
    n = nc + 2 * half + block
    n_row, n_col = lax.axis_size("row"), lax.axis_size("col")
    down = [(i, i + 1) for i in range(n_row - 1)]
    across = [((i - 1) % n_col, i) for i in range(n_col)]
    payload = jnp.concatenate(
        [coords, jnp.pad(coarse_coords, ((0, 0), (0, block - coarse_coords.shape[1])))], axis=0
    )
    held = exchanged(share_kernel, shape(n_row * n_col, 8, BLK), 0, payload)
    upper_values = lax.ppermute(values, "row", down)
    left_values = lax.ppermute(values, "col", across)
    all_values = lax.all_gather(coarse_values, ("row", "col"), axis=1, tiled=True)
    scale = jnp.exp(log_params[1:5]) * jnp.array(RANGE_BASE, F32)
    scal = jnp.concatenate(
        [jnp.exp(log_params[:1]), NUGGET * jnp.exp(log_params[5:]), 1.0 / scale]
    )
    row, col = lax.axis_index("row"), lax.axis_index("col")
    where = jnp.stack(
        [
            row * n_col + col,
            row,
            jnp.maximum(row - 1, 0) * n_col + col,
            row * n_col + lax.rem(col + n_col - 1, n_col),
        ]
    ).astype(jnp.int32)
    lead = n - block
    u, inv, wt, h, z, fish = pl.pallas_call(
        functools.partial(model_kernel, float(reps), coarse_coords.shape[1]),
        out_shape=[
            shape(n, n), shape(n, BLK), shape(n, BLK), shape(n, 5 * BLK), shape(BLK, 5 * BLK),
            shape(8, BLK),
        ],
        in_specs=[pl.BlockSpec(memory_space=pltpu.SMEM)] * 2 + vmem(3),
        out_specs=vmem(6),
        scratch_shapes=[
            pltpu.VMEM((n, n), F32), pltpu.VMEM((BLK, 2 * BLK), F32),
            pltpu.VMEM((8, n), F32), pltpu.VMEM((n, 8), F32),
        ],
        compiler_params=pltpu.CompilerParams(vmem_limit_bytes=40 * 1024 * 1024),
        cost_estimate=pl.CostEstimate(
            flops=60_000_000_000, bytes_accessed=8_000_000, transcendentals=2 * n * n
        ),
    )(scal, where, held, coarse_index, fine_index)
    white, terms = pl.pallas_call(
        data_kernel,
        out_shape=[shape(reps, BLK), shape(8, BLK)],
        in_specs=vmem(12),
        out_specs=vmem(2),
        scratch_shapes=[pltpu.VMEM((lead, BLK), F32)],
        compiler_params=pltpu.CompilerParams(vmem_limit_bytes=40 * 1024 * 1024),
    )(all_values, upper_values, left_values, values, coarse_index, fine_index, u, inv, wt, h, z, fish)
    solved = exchanged(solve_kernel, shape(8, BLK), 1, terms)
    return (solved[:6, 6], white)


def solution(mesh):
    in_specs = (
        P(None, ("row", "col")),
        P(None, ("row", "col")),
        P(None, ("row", "col")),
        P(None, ("row", "col")),
        P(("row", "col"), None),
        P(("row", "col"), None),
        P(),
    )
    out_specs = (P(), P(None, ("row", "col")))
    return jax.shard_map(body, mesh=mesh, in_specs=in_specs, out_specs=out_specs, check_vma=False)
```

```python
import functools
import math

import jax
import jax.numpy as jnp
from jax import lax
from jax.experimental import pallas as pl
from jax.experimental.pallas import tpu as pltpu
from jax.sharding import PartitionSpec as P

HIGH = lax.Precision.HIGHEST
ROOT_FIVE = math.sqrt(5.0)
NUGGET = 0.2
RANGE_BASE = (0.5, 0.5, 0.5, 0.5)
BLK = 128
PAN = 16
F32 = jnp.float32


def mm(a, b):
    return jnp.dot(a, b, precision=HIGH, preferred_element_type=F32)


def mm_tn(a, b):
    return lax.dot_general(
        a, b, (((0,), (0,)), ((), ())), precision=HIGH, preferred_element_type=F32
    )


def halves(x):
    high = x.astype(jnp.bfloat16)
    return high, (x - high.astype(F32)).astype(jnp.bfloat16)


def split_dot(a, b, dims):
    def dot(x, y):
        return lax.dot_general(x, y, (dims, ((), ())), preferred_element_type=F32)

    (ah, al), (bh, bl) = a, b
    return dot(ah, bh) + (dot(ah, bl) + dot(al, bh))


def mm3(a, b):
    return split_dot(halves(a), halves(b), ((1,), (0,)))


def mm3_tn(a, b):
    return split_dot(halves(a), halves(b), ((0,), (0,)))


def rows(b):
    return pl.ds(b * BLK, BLK)


def inverse_factor(s_ref):
    row = lax.broadcasted_iota(jnp.int32, (PAN, BLK), 0)
    lane = lax.broadcasted_iota(jnp.int32, (PAN, BLK), 1)

    def panel(p, carry):
        start = pl.multiple_of(p * PAN, PAN)
        xa = s_ref[pl.ds(start, PAN), :BLK]
        xb = s_ref[pl.ds(start, PAN), BLK:]
        turned = pltpu.roll(xa, lax.rem(BLK - start, BLK), 1)
        cols = [jnp.broadcast_to(turned[:, j : j + 1], (PAN, BLK)) for j in range(PAN)]
        for k in range(PAN):
            inv = lax.rsqrt(cols[k][k : k + 1, :])
            low = cols[k] * inv
            for j in range(k + 1, PAN):
                cols[j] = cols[j] - low * low[j : j + 1, :]
            below = jnp.where(row > k, low, 0.0)
            ua = xa[k : k + 1, :] * inv
            ub = xb[k : k + 1, :] * inv
            xa = jnp.where(row == k, ua, xa - below * ua)
            xb = jnp.where(row == k, ub, xb - below * ub)
        s_ref[pl.ds(start, PAN), :BLK] = xa
        s_ref[pl.ds(start, PAN), BLK:] = xb
        tail = jnp.where(lane >= start + PAN, xa, 0.0)
        s_ref[...] -= mm_tn(tail, jnp.concatenate([xa, xb], axis=1))
        return carry

    lax.fori_loop(0, BLK // PAN, panel, 0)


def forward(u_ref, inv_ref, x_ref, count):
    for b in range(count):
        part = x_ref[rows(b), :]
        if b:
            part = part - mm3_tn(u_ref[: b * BLK, b * BLK : (b + 1) * BLK], x_ref[: b * BLK, :])
        x_ref[rows(b), :] = mm3(inv_ref[rows(b), :], part)


def model_kernel(
    reps, per_tile, scal, where, held, cidx, fidx, u_ref, inv_ref, wt_ref, h_ref, z_ref, f_ref,
    c_ref, s_ref, xr, xc,
):
    n = xr.shape[1]
    nb = n // BLK
    lead = n - BLK
    lb = nb - 1
    nc = cidx.shape[1]
    half = fidx.shape[1] // 2
    count = held.shape[0]
    variance, nugget = scal[0], scal[1]
    row8 = lax.broadcasted_iota(jnp.int32, (8, BLK), 0)
    scale = sum(jnp.where(row8 == k, scal[2 + k], 0.0) for k in range(4))[:, :1]

    wanted = cidx[...]
    tile = wanted // per_tile
    spot = wanted - tile * per_tile
    hot = (lax.broadcasted_iota(jnp.int32, (BLK, nc), 0) == spot).astype(F32)
    spread = mm(held[...].reshape(count * 8, BLK), hot).reshape(count, 8, nc)
    owner = lax.broadcasted_iota(jnp.int32, (count, 8, nc), 0)
    coarse = jnp.sum(jnp.where(owner == tile[None], spread, 0.0), axis=0)
    xr[:, :nc] = pltpu.roll(coarse, 4, 0) * scale

    def neighbour(device, index):
        pick = (lax.broadcasted_iota(jnp.int32, (BLK, half), 0) == index).astype(F32)
        return mm(held[device], pick) * scale

    alive = jnp.where(where[1] > 0, 1.0, 0.0)
    near = jnp.concatenate(
        [neighbour(where[2], fidx[:, :half]) * alive, neighbour(where[3], fidx[:, half:])], axis=1
    )
    xr[:, nc:lead] = near
    xr[:, lead:] = held[where[0]] * scale
    point = lax.broadcasted_iota(jnp.int32, (1, n), 1)
    xr[4:5, :] = jnp.where((point >= nc) & (point < nc + half), alive, 1.0)
    for b in range(nb):
        xc[rows(b), :] = xr[:, b * BLK : (b + 1) * BLK].T

    def cover(r, carry):
        start = pl.multiple_of(r * 64, 64)
        here = pl.ds(start, 64)
        total = None
        for k in range(4):
            diff = xc[here, k : k + 1] - xr[k : k + 1, :]
            total = diff * diff if total is None else total + diff * diff
        live_c = xc[here, 4:5]
        paired = live_c * xr[4:5, :]
        root = ROOT_FIVE * jnp.sqrt(total)
        decay = jnp.exp(-root) * (variance * paired)
        ident = (
            lax.broadcasted_iota(jnp.int32, (64, n), 0) + start
            == lax.broadcasted_iota(jnp.int32, (64, n), 1)
        )
        u_ref[here, :] = (1.0 + root + root * root / 3.0) * decay + jnp.where(
            ident, live_c * nugget + 1.0 - live_c, 0.0
        )
        c_ref[here, :] = (5.0 / 3.0) * (1.0 + root) * decay
        return carry

    lax.fori_loop(0, n // 64, cover, 0)

    eye = (
        lax.broadcasted_iota(jnp.int32, (BLK, BLK), 0)
        == lax.broadcasted_iota(jnp.int32, (BLK, BLK), 1)
    ).astype(F32)
    for b in range(nb):
        s_ref[:, :BLK] = u_ref[rows(b), b * BLK : (b + 1) * BLK]
        s_ref[:, BLK:] = eye
        inverse_factor(s_ref)
        inv = s_ref[:, BLK:]
        inv_ref[rows(b), :] = inv
        if b + 1 < nb:
            rest = (b + 1) * BLK
            u_ref[rows(b), rest:] = mm(inv, u_ref[rows(b), rest:])
            for i in range(b + 1, nb):
                u_ref[rows(i), i * BLK :] -= mm_tn(
                    u_ref[rows(b), i * BLK : (i + 1) * BLK], u_ref[rows(b), i * BLK :]
                )

    last = inv_ref[rows(lb), :]
    wt_ref[rows(lb), :] = last.T
    right = -mm(u_ref[:lead, lead:], last.T)
    for b in range(lb - 1, -1, -1):
        part = right[b * BLK : (b + 1) * BLK, :]
        if b + 1 < lb:
            part = part - mm(u_ref[rows(b), (b + 1) * BLK : lead], wt_ref[(b + 1) * BLK : lead, :])
        wt_ref[rows(b), :] = mm_tn(inv_ref[rows(b), :], part)

    wt = halves(wt_ref[...])

    def slopes(r, carry):
        here = pl.ds(pl.multiple_of(r * BLK, BLK), BLK)
        for k in range(4):
            diff = xc[here, k : k + 1] - xr[k : k + 1, :]
            h_ref[here, k * BLK : (k + 1) * BLK] = split_dot(
                halves(c_ref[here, :] * (diff * diff)), wt, ((1,), (0,))
            )
        h_ref[here, 4 * BLK :] = nugget * wt_ref[here, :]
        return carry

    lax.fori_loop(0, nb, slopes, 0)
    z_ref[...] = split_dot(wt, halves(h_ref[...]), ((0,), (0,)))
    forward(u_ref, inv_ref, h_ref, lb)

    def h_of(i):
        i = 4 if i in (0, 5) else i - 1
        return h_ref[:lead, i * BLK : (i + 1) * BLK]

    def z_of(i):
        if i == 0:
            return eye - z_ref[:, 4 * BLK :]
        return z_ref[:, (i - 1) * BLK : i * BLK]

    lane8 = lax.broadcasted_iota(jnp.int32, (8, BLK), 1)
    out = jnp.zeros((8, BLK), F32)
    for i in range(6):
        for j in range(i, 6):
            sign = -2.0 if (i == 0) != (j == 0) else 2.0
            both = sign * jnp.sum(h_of(i) * h_of(j), axis=0, keepdims=True)
            both = both + jnp.sum(z_of(i) * z_of(j), axis=0, keepdims=True)
            value = (0.5 * reps) * jnp.sum(both, axis=1, keepdims=True)
            spot = (row8 == i) & (lane8 == j) | (row8 == j) & (lane8 == i)
            out = out + jnp.where(spot, value, 0.0)
    f_ref[...] = out


def data_kernel(
    coarse, upper, left, own, cidx, fidx, u_ref, inv_ref, wt_ref, h_ref, z_ref, f_ref,
    white_ref, out_ref, m_ref,
):
    reps = own.shape[0]
    n = wt_ref.shape[0]
    lead = n - BLK
    nc = cidx.shape[1]
    half = fidx.shape[1] // 2

    def onehot(index, count):
        return (
            lax.broadcasted_iota(jnp.int32, (count, index.shape[1]), 0) == index
        ).astype(F32)

    hot_c = onehot(cidx[...], coarse.shape[1])
    hot_u = onehot(fidx[:, :half], upper.shape[1])
    hot_l = onehot(fidx[:, half:], left.shape[1])
    white = mm3(coarse[...], mm3(hot_c, wt_ref[:nc, :]))
    white = white + mm3(upper[...], mm3(hot_u, wt_ref[nc : nc + half, :]))
    white = white + mm3(left[...], mm3(hot_l, wt_ref[nc + half : lead, :]))
    white = white + mm3(own[...], wt_ref[lead:, :])
    white_ref[...] = white
    m_ref[:nc, :] = mm3_tn(hot_c, mm3_tn(coarse[...], white))
    m_ref[nc : nc + half, :] = mm3_tn(hot_u, mm3_tn(upper[...], white))
    m_ref[nc + half :, :] = mm3_tn(hot_l, mm3_tn(left[...], white))
    forward(u_ref, inv_ref, m_ref, lead // BLK)
    gram = mm3_tn(white, white)
    eye = (
        lax.broadcasted_iota(jnp.int32, (BLK, BLK), 0)
        == lax.broadcasted_iota(jnp.int32, (BLK, BLK), 1)
    ).astype(F32)
    weight = 0.5 * gram - (0.5 * reps) * eye
    row8 = lax.broadcasted_iota(jnp.int32, (8, BLK), 0)
    lane8 = lax.broadcasted_iota(jnp.int32, (8, BLK), 1)
    out = f_ref[...]
    for i in range(6):
        at = 4 if i in (0, 5) else i - 1
        lead_part = jnp.sum(m_ref[...] * h_ref[:lead, at * BLK : (at + 1) * BLK], axis=0, keepdims=True)
        z = z_ref[:, at * BLK : (at + 1) * BLK]
        if i == 0:
            z = eye - z
            lead_part = -lead_part
        both = lead_part + jnp.sum(weight * z, axis=0, keepdims=True)
        value = jnp.sum(both, axis=1, keepdims=True)
        out = out + jnp.where((row8 == i) & (lane8 == 6), value, 0.0)
    out_ref[...] = out


def exchange(x_ref, held, send_sem, recv_sem):
    n_row, n_col = lax.axis_size("row"), lax.axis_size("col")
    count = n_row * n_col
    me = lax.axis_index("row") * n_col + lax.axis_index("col")

    def place(device):
        return {"row": device // n_col, "col": lax.rem(device, n_col)}

    barrier = pltpu.get_barrier_semaphore()

    def greet(d, carry):
        pl.semaphore_signal(
            barrier, inc=1, device_id=place(lax.rem(me + d, count)),
            device_id_type=pl.DeviceIdType.MESH,
        )
        return carry

    lax.fori_loop(1, count, greet, 0)
    pl.semaphore_wait(barrier, count - 1)

    def copy(d, slot):
        return pltpu.make_async_remote_copy(
            src_ref=x_ref, dst_ref=held.at[slot], send_sem=send_sem.at[d],
            recv_sem=recv_sem.at[d], device_id=place(lax.rem(me + d, count)),
            device_id_type=pl.DeviceIdType.MESH,
        )

    def push(d, carry):
        copy(d, me).start()
        return carry

    def settle(d, carry):
        copy(d, lax.rem(me - d + count, count)).wait()
        return carry

    lax.fori_loop(1, count, push, 0)
    held[me] = x_ref[...]
    lax.fori_loop(1, count, settle, 0)


def share_kernel(x_ref, out_ref, held, send_sem, recv_sem):
    exchange(x_ref, held, send_sem, recv_sem)
    out_ref[...] = held[...]


def solve_kernel(x_ref, out_ref, held, send_sem, recv_sem):
    exchange(x_ref, held, send_sem, recv_sem)
    out_ref[...] = eliminated(jnp.sum(held[...], axis=0))


def exchanged(kernel, out_shape, number, payload):
    count = lax.axis_size("row") * lax.axis_size("col")
    return pl.pallas_call(
        kernel,
        out_shape=out_shape,
        in_specs=vmem(1),
        out_specs=vmem(1)[0],
        scratch_shapes=[
            pltpu.VMEM((count, 8, BLK), F32),
            pltpu.SemaphoreType.DMA((count,)),
            pltpu.SemaphoreType.DMA((count,)),
        ],
        compiler_params=pltpu.CompilerParams(collective_id=number, has_side_effects=True),
    )(payload)


def eliminated(x):
    row8 = lax.broadcasted_iota(jnp.int32, (8, BLK), 0)
    for k in range(6):
        top = x[k : k + 1, :] / x[k : k + 1, k : k + 1]
        x = jnp.where(row8 == k, top, x - x[:, k : k + 1] * top)
    return x


def vmem(count):
    return [pl.BlockSpec(memory_space=pltpu.VMEM)] * count


def shape(*dims):
    return jax.ShapeDtypeStruct(dims, F32)


def body(coords, values, coarse_coords, coarse_values, fine_index, coarse_index, log_params):
    half = fine_index.shape[1] // 2
    reps = values.shape[0]
    block = coords.shape[1]
    nc = coarse_index.shape[1]
    n = nc + 2 * half + block
    n_row, n_col = lax.axis_size("row"), lax.axis_size("col")
    down = [(i, i + 1) for i in range(n_row - 1)]
    across = [((i - 1) % n_col, i) for i in range(n_col)]
    payload = jnp.concatenate(
        [coords, jnp.pad(coarse_coords, ((0, 0), (0, block - coarse_coords.shape[1])))], axis=0
    )
    held = exchanged(share_kernel, shape(n_row * n_col, 8, BLK), 0, payload)
    upper_values = lax.ppermute(values, "row", down)
    left_values = lax.ppermute(values, "col", across)
    all_values = lax.all_gather(coarse_values, ("row", "col"), axis=1, tiled=True)
    scale = jnp.exp(log_params[1:5]) * jnp.array(RANGE_BASE, F32)
    scal = jnp.concatenate(
        [jnp.exp(log_params[:1]), NUGGET * jnp.exp(log_params[5:]), 1.0 / scale]
    )
    row, col = lax.axis_index("row"), lax.axis_index("col")
    where = jnp.stack(
        [
            row * n_col + col,
            row,
            jnp.maximum(row - 1, 0) * n_col + col,
            row * n_col + lax.rem(col + n_col - 1, n_col),
        ]
    ).astype(jnp.int32)
    lead = n - block
    u, inv, wt, h, z, fish = pl.pallas_call(
        functools.partial(model_kernel, float(reps), coarse_coords.shape[1]),
        out_shape=[
            shape(n, n), shape(n, BLK), shape(n, BLK), shape(n, 5 * BLK), shape(BLK, 5 * BLK),
            shape(8, BLK),
        ],
        in_specs=[pl.BlockSpec(memory_space=pltpu.SMEM)] * 2 + vmem(3),
        out_specs=vmem(6),
        scratch_shapes=[
            pltpu.VMEM((n, n), F32), pltpu.VMEM((BLK, 2 * BLK), F32),
            pltpu.VMEM((8, n), F32), pltpu.VMEM((n, 8), F32),
        ],
        compiler_params=pltpu.CompilerParams(vmem_limit_bytes=16 * 1024 * 1024),
        cost_estimate=pl.CostEstimate(
            flops=60_000_000_000, bytes_accessed=8_000_000, transcendentals=2 * n * n
        ),
    )(scal, where, held, coarse_index, fine_index)
    white, terms = pl.pallas_call(
        data_kernel,
        out_shape=[shape(reps, BLK), shape(8, BLK)],
        in_specs=vmem(12),
        out_specs=vmem(2),
        scratch_shapes=[pltpu.VMEM((lead, BLK), F32)],
        compiler_params=pltpu.CompilerParams(vmem_limit_bytes=16 * 1024 * 1024),
    )(all_values, upper_values, left_values, values, coarse_index, fine_index, u, inv, wt, h, z, fish)
    solved = exchanged(solve_kernel, shape(8, BLK), 1, terms)
    return (solved[:6, 6], white)


def solution(mesh):
    in_specs = (
        P(None, ("row", "col")),
        P(None, ("row", "col")),
        P(None, ("row", "col")),
        P(None, ("row", "col")),
        P(("row", "col"), None),
        P(("row", "col"), None),
        P(),
    )
    out_specs = (P(), P(None, ("row", "col")))
    return jax.shard_map(body, mesh=mesh, in_specs=in_specs, out_specs=out_specs, check_vma=False)
```
